32 devices in a mesh: dp: 2 (over y), table: 16 (over z, x, core).
Axes of the slice: x: 2, y: 2, z: 4, core: 2. Of those that a mesh axis runs over, the one named last changes fastest.
Arguments:
- gradients: bfloat16 [256, 4096], P(None, ('dp', 'table')), may hold values from -16 to 16
- row_ids: int32 [4096], P(('dp', 'table')), may hold values from 0 to 32767
- table_block: float32 [256, 32768], P('table', 'dp'), may hold values from -6 to 6
- adagrad_state: float32 [32768], P('dp'), may hold values from 0.05 to 2
Outputs:
- new_table: float32 [256, 32768], P('table', 'dp')
- new_state: float32 [32768], P('dp')
The draws below stay inside these ranges and needn't reach their ends.
All inputs are finite; a program needn't handle non-finite values.
Results may differ from the reference program's by a relative error of at most 0.0003.
Values may be sent and summed in bfloat16 or wider, within the bound.
A program may use at most 64 MiB of HBM per device.

```python
import math
import jax
import jax.numpy as jnp
from jax import lax

W = 256
TILE = 128
ROWS = 32768
LOOKUPS = 4096
TILES = 256


def draw_gradients(key, part):
    first, second = jax.random.split(key, 2)
    rising = 3.0 ** (jnp.arange(W, dtype=jnp.float32) / (W - 1))
    jitter = jnp.exp(jax.random.uniform(second, (W,), jnp.float32, 0.0, math.log(4.0)))
    column = 0.4 * rising * jitter
    values = jax.random.normal(first, (W, LOOKUPS), jnp.float32) * column[:, None]
    return jnp.clip(values, -16.0, 16.0).astype(jnp.bfloat16)


def draw_row_ids(key, part):
    first, second, third = jax.random.split(key, 3)
    heat = jax.random.randint(first, (TILES,), 0, 4)
    weight = jnp.where(heat == 0, 4, 1).astype(jnp.int32)
    cumulative = jnp.cumsum(weight)
    picked = jax.random.randint(second, (LOOKUPS,), 0, cumulative[-1])
    tile_index = jnp.searchsorted(cumulative, picked, side='right').astype(jnp.int32)
    offset = jax.random.randint(third, (LOOKUPS,), 0, TILE)
    result = tile_index * TILE + offset
    result = result.at[0].set(0).at[1].set(ROWS - 1)
    return result.astype(jnp.int32)


def level_of(stream_key, shape, pieces, smallest, largest):
    loudness, own = 1.0, jax.random.fold_in(stream_key, 6)
    for dim, parts in pieces:
        draws = jnp.exp(jax.random.uniform(jax.random.fold_in(own, dim), (parts,), jnp.float32, smallest / len(pieces), largest / len(pieces)))
        loudness = loudness * jnp.repeat(draws, shape[dim] // parts).reshape([-1 if axis == dim else 1 for axis in range(len(shape))])
    return loudness


def gaussian(stream_key, dims, spread, limit, shards=(), kind=jnp.bfloat16):
    level = level_of(stream_key, dims, shards, -0.22, 0.18) if shards else 1.0
    values = jax.random.normal(stream_key, dims, jnp.float32) * spread * level
    return jnp.minimum(jnp.maximum(values, -limit), limit).astype(kind)


def setup_inputs(seed: int = 0) -> dict:
    key_of = jax.random.split(jax.random.key(seed), 5)
    return {
        "gradients": draw_gradients(jax.random.fold_in(key_of[4], 71), 0),
        "row_ids": draw_row_ids(jax.random.fold_in(key_of[4], 71), 0),
        "table_block": gaussian(key_of[2], (W, ROWS), 1.0, 6.0, ((0, 16), (1, 2)), jnp.float32),
        "adagrad_state": jnp.clip(jnp.exp(math.log(2.0) - 3.6888794 * jax.random.uniform(key_of[3], (ROWS,), jnp.float32) ** level_of(key_of[3], (ROWS,), ((0, 2),), -0.2, 0.2)), 0.05, 2.0),
    }


learn_rate = 0.5

def reference(gradients, row_ids, table_block, adagrad_state):
    zeros = jnp.zeros((W, ROWS), jnp.float32)
    row_grad = zeros.at[:, row_ids].add(gradients.astype(jnp.float32))
    new_state = adagrad_state + lax.optimization_barrier(jnp.sum(row_grad * row_grad, axis=0)) / W
    new_table = table_block - learn_rate * row_grad / jnp.sqrt(new_state)[None, :]
    return (new_table, new_state)
```

```python
import functools

import jax
import jax.numpy as jnp
from jax import lax
from jax.experimental import pallas as pl
from jax.experimental.pallas import tpu as pltpu
from jax.sharding import PartitionSpec as P

learn_rate = 0.5
LO = 256
LANES = 128
MESH = pl.DeviceIdType.MESH


def accumulate(grads, ids, first_row, count_rows):
    relative = ids - first_row
    inside = (relative >= 0) & (relative < count_rows)
    target = jnp.where(inside, relative, count_rows)
    start_total = jnp.zeros((grads.shape[0], count_rows), jnp.float32)
    return start_total.at[:, target].add(grads.astype(jnp.float32), mode="drop")


def plain_body(width, gradients, row_ids, table_block, adagrad_state):
    owned = lax.all_to_all(gradients, "table", split_axis=0, concat_axis=1, tiled=True)
    local_rows = table_block.shape[1]
    all_row_ids = lax.all_gather(row_ids, ("dp", "table"), axis=0, tiled=True)
    first_row = lax.axis_index("dp") * local_rows
    row_grad = accumulate(
        lax.all_gather(owned, "dp", axis=1, tiled=True), all_row_ids, first_row, local_rows
    )
    partial_squares = jnp.sum(row_grad * row_grad, axis=0)
    squares = lax.psum(partial_squares, "table")
    new_state = adagrad_state + squares / width
    new_table = table_block - learn_rate * row_grad / jnp.sqrt(new_state)[None, :]
    return (new_table, new_state)


def exchange_kernel(
    dp, tb, cols, rows,
    g_ref, id_ref, acc_out, sq_ref,
    acc, got_g, got_i, part, red, total, full,
    send_g, send_i, send_r, send_a, recv_g, recv_i, recv_r, recv_a, own_sem, acc_sem,
):
    d, t = lax.axis_index("dp"), lax.axis_index("table")
    n = dp * tb
    me = d * tb + t
    his = rows // LO
    first_row = d * rows

    barrier = pltpu.get_barrier_semaphore()

    @pl.loop(1, n)
    def _(k):
        peer = lax.rem(me + k, n)
        pl.semaphore_signal(
            barrier, inc=1, device_id=(peer // tb, lax.rem(peer, tb)), device_id_type=MESH
        )

    own_g = pltpu.make_async_copy(g_ref.at[t], got_g.at[me], own_sem.at[0])
    own_i = pltpu.make_async_copy(id_ref, got_i.at[me], own_sem.at[1])
    own_g.start()
    own_i.start()
    acc[...] = jnp.zeros_like(acc)
    pl.semaphore_wait(barrier, n - 1)

    def block_copies(k):
        peer = lax.rem(me + k, n)
        to = (peer // tb, lax.rem(peer, tb))
        return (
            pltpu.make_async_remote_copy(
                src_ref=id_ref, dst_ref=got_i.at[me],
                send_sem=send_i.at[peer], recv_sem=recv_i.at[me],
                device_id=to, device_id_type=MESH,
            ),
            pltpu.make_async_remote_copy(
                src_ref=g_ref.at[to[1]], dst_ref=got_g.at[me],
                send_sem=send_g.at[peer], recv_sem=recv_g.at[me],
                device_id=to, device_id_type=MESH,
            ),
        )

    @pl.loop(1, n)
    def _(k):
        for copy in block_copies(k):
            copy.start()

    own_g.wait()
    own_i.wait()

    @pl.loop(1, n)
    def _(k):
        source = lax.rem(me + k, n)
        pltpu.make_async_copy(id_ref, got_i.at[source], recv_i.at[source]).wait()
        pltpu.make_async_copy(g_ref.at[t], got_g.at[source], recv_g.at[source]).wait()

    @pl.loop(0, n // 2)
    def _(k):
        ids = jnp.concatenate([got_i[2 * k], got_i[2 * k + 1]], axis=1) - first_row
        grads = jnp.concatenate([got_g[2 * k], got_g[2 * k + 1]], axis=1)
        span = ids.shape[1]
        low = jnp.broadcast_to(lax.bitwise_and(ids, LO - 1), (LO, span))
        place = lax.broadcasted_iota(jnp.int32, (LO, span), 0)
        one_hot = jnp.where(low == place, 1.0, 0.0).astype(jnp.bfloat16)
        high = jnp.broadcast_to(lax.shift_right_arithmetic(ids, 8), (cols, span))
        wide = grads.astype(jnp.float32)
        picked = jnp.concatenate(
            [jnp.where(high == h, wide, 0.0).astype(jnp.bfloat16) for h in range(his)], axis=0
        )
        acc[...] += lax.dot_general(
            picked, one_hot, (((1,), (1,)), ((), ())), preferred_element_type=jnp.float32
        )

    out_copy = pltpu.make_async_copy(acc, acc_out, acc_sem)
    out_copy.start()

    each = his // tb

    @pl.loop(0, tb)
    def _(j):
        lines = []
        for h in range(each):
            at = pl.multiple_of((j * each + h) * cols, cols)
            piece = acc[pl.ds(at, cols), :]
            sums = jnp.sum(piece * piece, axis=0, keepdims=True)
            for half in range(LO // LANES):
                lines.append(sums[:, half * LANES:(half + 1) * LANES])
        part[j] = jnp.concatenate(lines, axis=0)

    @pl.loop(1, tb)
    def _(k):
        to = lax.rem(t + k, tb)
        pltpu.make_async_remote_copy(
            src_ref=part.at[to], dst_ref=red.at[t],
            send_sem=send_r.at[to], recv_sem=recv_r.at[t],
            device_id=(d, to), device_id_type=MESH,
        ).start()

    @pl.loop(1, tb)
    def _(k):
        source = lax.rem(t + k, tb)
        pltpu.make_async_copy(part.at[t], red.at[source], recv_r.at[source]).wait()

    red[t] = part[t]
    total[...] = jnp.sum(red[...], axis=0)
    full[t] = total[...]

    @pl.loop(1, tb)
    def _(k):
        to = lax.rem(t + k, tb)
        pltpu.make_async_remote_copy(
            src_ref=total, dst_ref=full.at[t],
            send_sem=send_a.at[to], recv_sem=recv_a.at[t],
            device_id=(d, to), device_id_type=MESH,
        ).start()

    @pl.loop(1, n)
    def _(k):
        for copy in block_copies(k):
            copy.wait_send()

    @pl.loop(1, tb)
    def _(k):
        to = lax.rem(t + k, tb)
        pltpu.make_async_copy(part.at[to], red.at[t], send_r.at[to]).wait()
        pltpu.make_async_copy(total, full.at[t], send_a.at[to]).wait()

    @pl.loop(1, tb)
    def _(k):
        source = lax.rem(t + k, tb)
        pltpu.make_async_copy(total, full.at[source], recv_a.at[source]).wait()

    sq_ref[...] = full[...]
    out_copy.wait()


def update_kernel(width, cols, acc_ref, sq_ref, state_ref, table_ref, table_out, state_out):
    state = state_ref[...] + sq_ref[...] / width
    state_out[...] = state
    scale = learn_rate / jnp.sqrt(state)
    parts = LO // LANES
    for r in range(scale.shape[0]):
        h, half = r // parts, r % parts
        lanes = slice(r * LANES, (r + 1) * LANES)
        step = acc_ref[h * cols:(h + 1) * cols, half * LANES:(half + 1) * LANES]
        table_out[:, lanes] = table_ref[:, lanes] - step * scale[r:r + 1, :]


def kernel_body(dp, tb, width, gradients, row_ids, table_block, adagrad_state):
    cols, rows = table_block.shape
    count = row_ids.shape[0]
    n = dp * tb
    his = rows // LO
    lines = rows // tb // LANES
    dma = pltpu.SemaphoreType.DMA
    acc, squares = pl.pallas_call(
        functools.partial(exchange_kernel, dp, tb, cols, rows),
        name="exchange",
        out_shape=(
            jax.ShapeDtypeStruct((his * cols, LO), jnp.float32),
            jax.ShapeDtypeStruct((tb, lines, LANES), jnp.float32),
        ),
        in_specs=[pl.BlockSpec(memory_space=pl.ANY)] * 2,
        out_specs=(
            pl.BlockSpec(memory_space=pl.ANY),
            pl.BlockSpec(memory_space=pltpu.VMEM),
        ),
        scratch_shapes=[
            pltpu.VMEM((his * cols, LO), jnp.float32),
            pltpu.VMEM((n, cols, count), jnp.bfloat16),
            pltpu.VMEM((n, 1, count), jnp.int32),
            pltpu.VMEM((tb, lines, LANES), jnp.float32),
            pltpu.VMEM((tb, lines, LANES), jnp.float32),
            pltpu.VMEM((lines, LANES), jnp.float32),
            pltpu.VMEM((tb, lines, LANES), jnp.float32),
            dma((n,)), dma((n,)), dma((tb,)), dma((tb,)),
            dma((n,)), dma((n,)), dma((tb,)), dma((tb,)),
            dma((2,)), dma,
        ],
        compiler_params=pltpu.CompilerParams(collective_id=0, has_side_effects=True),
    )(gradients.reshape(tb, cols, count), row_ids.reshape(1, count))

    steps = 4
    block = rows // steps
    flat = (rows // LANES, LANES)
    line_spec = pl.BlockSpec((block // LANES, LANES), lambda i: (i, 0))
    wide_spec = pl.BlockSpec((cols, block), lambda i: (0, i))
    new_table, new_state = pl.pallas_call(
        functools.partial(update_kernel, width, cols),
        name="update",
        grid=(steps,),
        out_shape=(
            jax.ShapeDtypeStruct((cols, rows), jnp.float32),
            jax.ShapeDtypeStruct(flat, jnp.float32),
        ),
        in_specs=[
            pl.BlockSpec((his * cols // steps, LO), lambda i: (i, 0)),
            line_spec, line_spec, wide_spec,
        ],
        out_specs=(wide_spec, line_spec),
    )(acc, squares.reshape(flat), adagrad_state.reshape(flat), table_block)
    return (new_table, new_state.reshape(rows))


def body(dp, tb, gradients, row_ids, table_block, adagrad_state):
    width = gradients.shape[0]
    cols, rows = table_block.shape
    fits = (
        cols % 16 == 0
        and rows % (tb * 8 * LANES) == 0
        and rows % (4 * LO * 4) == 0
        and (dp * tb) % 2 == 0
        and row_ids.shape[0] == LANES
    )
    args = (gradients, row_ids, table_block, adagrad_state)
    if fits:
        return kernel_body(dp, tb, width, *args)
    return plain_body(width, *args)


def solution(mesh):
    in_specs = (P(None, ("dp", "table")), P(("dp", "table")), P("table", "dp"), P("dp"))
    out_specs = (P("table", "dp"), P("dp"))
    run = functools.partial(body, mesh.shape["dp"], mesh.shape["table"])
    return jax.shard_map(run, mesh=mesh, in_specs=in_specs, out_specs=out_specs, check_vma=False)
```

```python
import functools

import jax
import jax.numpy as jnp
from jax import lax
from jax.experimental import pallas as pl
from jax.experimental.pallas import tpu as pltpu
from jax.sharding import PartitionSpec as P

learn_rate = 0.5
LO = 256
LANES = 128
MESH = pl.DeviceIdType.MESH


def accumulate(grads, ids, first_row, count_rows):
    relative = ids - first_row
    inside = (relative >= 0) & (relative < count_rows)
    target = jnp.where(inside, relative, count_rows)
    start_total = jnp.zeros((grads.shape[0], count_rows), jnp.float32)
    return start_total.at[:, target].add(grads.astype(jnp.float32), mode="drop")


def plain_body(width, gradients, row_ids, table_block, adagrad_state):
    owned = lax.all_to_all(gradients, "table", split_axis=0, concat_axis=1, tiled=True)
    local_rows = table_block.shape[1]
    all_row_ids = lax.all_gather(row_ids, ("dp", "table"), axis=0, tiled=True)
    first_row = lax.axis_index("dp") * local_rows
    row_grad = accumulate(
        lax.all_gather(owned, "dp", axis=1, tiled=True), all_row_ids, first_row, local_rows
    )
    partial_squares = jnp.sum(row_grad * row_grad, axis=0)
    squares = lax.psum(partial_squares, "table")
    new_state = adagrad_state + squares / width
    new_table = table_block - learn_rate * row_grad / jnp.sqrt(new_state)[None, :]
    return (new_table, new_state)


def flip(value, by, size):
    out, bit = 0, 1
    while bit < size:
        out = out + lax.rem(value // bit + by // bit, 2) * bit
        bit *= 2
    return out


def exchange_kernel(
    dp, tb, cols, rows, width,
    g_ref, id_ref, state_ref, table_ref, table_out, state_out,
    acc, got_g, got_i, table, part, red, total, full, state,
    send_g, send_i, send_r, send_a, recv_g, recv_i, recv_r, recv_a, own_sem,
):
    d, t = lax.axis_index("dp"), lax.axis_index("table")
    n = dp * tb
    me = d * tb + t
    his = rows // LO
    lines = rows // tb // LANES
    parts = LO // LANES
    first_row = d * rows

    def device(k):
        side = flip(t, lax.rem(k, 4) + (k // (4 * dp)) * 4, tb)
        return flip(d, lax.rem(k // 4, dp), dp), side

    barrier = pltpu.get_barrier_semaphore()

    @pl.loop(1, n)
    def _(k):
        pl.semaphore_signal(barrier, inc=1, device_id=device(n - k), device_id_type=MESH)

    own = (
        pltpu.make_async_copy(g_ref.at[t], got_g.at[me], own_sem.at[0]),
        pltpu.make_async_copy(id_ref, got_i.at[me], own_sem.at[1]),
        pltpu.make_async_copy(state_ref, state, own_sem.at[2]),
        pltpu.make_async_copy(table_ref, table, own_sem.at[3]),
    )
    for copy in own:
        copy.start()
    acc[...] = jnp.zeros_like(acc)
    pl.semaphore_wait(barrier, n - 1)

    def block_copies(k):
        to = device(k)
        peer = to[0] * tb + to[1]
        return (
            pltpu.make_async_remote_copy(
                src_ref=id_ref, dst_ref=got_i.at[me],
                send_sem=send_i.at[peer], recv_sem=recv_i.at[me],
                device_id=to, device_id_type=MESH,
            ),
            pltpu.make_async_remote_copy(
                src_ref=g_ref.at[to[1]], dst_ref=got_g.at[me],
                send_sem=send_g.at[peer], recv_sem=recv_g.at[me],
                device_id=to, device_id_type=MESH,
            ),
        )

    @pl.loop(1, n)
    def _(k):
        for copy in block_copies(k):
            copy.start()

    def arrived(k):
        there = device(k)
        source = there[0] * tb + there[1]
        pltpu.make_async_copy(id_ref, got_i.at[source], recv_i.at[source]).wait()
        pltpu.make_async_copy(g_ref.at[t], got_g.at[source], recv_g.at[source]).wait()
        return source

    def add(sources):
        ids = jnp.concatenate([got_i[k] for k in sources], axis=1) - first_row
        grads = jnp.concatenate([got_g[k] for k in sources], axis=1)
        span = ids.shape[1]
        low = jnp.broadcast_to(lax.bitwise_and(ids, LO - 1), (LO, span))
        place = lax.broadcasted_iota(jnp.int32, (LO, span), 0)
        one_hot = jnp.where(low == place, 1.0, 0.0).astype(jnp.bfloat16)
        high = jnp.broadcast_to(lax.shift_right_arithmetic(ids, 8), (cols, span))
        high = jnp.clip(high, -1, his).astype(jnp.float32).astype(jnp.bfloat16)
        zero = jnp.zeros_like(grads)
        picked = jnp.concatenate(
            [jnp.where(high == jnp.bfloat16(h), grads, zero) for h in range(his)], axis=0
        )
        acc[...] += lax.dot_general(
            picked, one_hot, (((1,), (1,)), ((), ())), preferred_element_type=jnp.float32
        )

    own[0].wait()
    own[1].wait()
    GROUP = 4
    add([me] + [arrived(k) for k in range(1, GROUP)])

    @pl.loop(1, n // GROUP)
    def _(k):
        add([arrived(GROUP * k + i) for i in range(GROUP)])

    each = his // tb
    for j in range(tb):
        pieces = []
        for h in range(each):
            at = (j * each + h) * cols
            piece = acc[at:at + cols, :]
            sums = jnp.sum(piece * piece, axis=0, keepdims=True)
            for half in range(parts):
                pieces.append(sums[:, half * LANES:(half + 1) * LANES])
        part[j] = jnp.concatenate(pieces, axis=0)

    @pl.loop(1, tb)
    def _(k):
        to = flip(t, tb - k, tb)
        pltpu.make_async_remote_copy(
            src_ref=part.at[to], dst_ref=red.at[t],
            send_sem=send_r.at[to], recv_sem=recv_r.at[t],
            device_id=(d, to), device_id_type=MESH,
        ).start()

    own[2].wait()
    own[3].wait()
    red[t] = part[t]

    @pl.loop(1, tb)
    def _(k):
        source = flip(t, k, tb)
        pltpu.make_async_copy(part.at[t], red.at[source], recv_r.at[source]).wait()

    here = pl.ds(pl.multiple_of(t * lines, lines), lines)
    total[...] = state[here, :] + jnp.sum(red[...], axis=0) / width
    full[t] = total[...]

    @pl.loop(1, tb)
    def _(k):
        to = flip(t, tb - k, tb)
        pltpu.make_async_copy(part.at[to], red.at[t], send_r.at[to]).wait()

    @pl.loop(1, tb)
    def _(k):
        to = flip(t, tb - k, tb)
        pltpu.make_async_remote_copy(
            src_ref=total, dst_ref=full.at[t],
            send_sem=send_a.at[to], recv_sem=recv_a.at[t],
            device_id=(d, to), device_id_type=MESH,
        ).start()

    def update(j):
        fresh = full[j]
        state_out[j] = fresh
        scale = learn_rate / jnp.sqrt(fresh)
        for r in range(lines):
            h, half = r // parts, r % parts
            at = pl.multiple_of((j * each + h) * cols, cols)
            lanes = pl.ds(pl.multiple_of((j * lines + r) * LANES, LANES), LANES)
            step = acc[pl.ds(at, cols), half * LANES:(half + 1) * LANES]
            table_out[:, lanes] = table[:, lanes] - step * scale[r:r + 1, :]

    @pl.loop(1, n)
    def _(k):
        for copy in block_copies(k):
            copy.wait_send()

    update(t)

    @pl.loop(1, tb)
    def _(k):
        source = flip(t, k, tb)
        pltpu.make_async_copy(total, full.at[source], recv_a.at[source]).wait()
        update(source)

    @pl.loop(1, tb)
    def _(k):
        to = flip(t, tb - k, tb)
        pltpu.make_async_copy(total, full.at[t], send_a.at[to]).wait()


def kernel_body(dp, tb, width, gradients, row_ids, table_block, adagrad_state):
    cols, rows = table_block.shape
    count = row_ids.shape[0]
    n = dp * tb
    his = rows // LO
    lines = rows // tb // LANES
    dma = pltpu.SemaphoreType.DMA
    new_table, new_state = pl.pallas_call(
        functools.partial(exchange_kernel, dp, tb, cols, rows, width),
        name="exchange",
        out_shape=(
            pltpu.VMEM((cols, rows), jnp.float32),
            pltpu.VMEM((tb, lines, LANES), jnp.float32),
        ),
        in_specs=[pl.BlockSpec(memory_space=pl.ANY)] * 4,
        out_specs=(pl.BlockSpec(memory_space=pltpu.VMEM),) * 2,
        scratch_shapes=[
            pltpu.VMEM((his * cols, LO), jnp.float32),
            pltpu.VMEM((n, cols, count), jnp.bfloat16),
            pltpu.VMEM((n, 1, count), jnp.int32),
            pltpu.VMEM((cols, rows), jnp.float32),
            pltpu.VMEM((tb, lines, LANES), jnp.float32),
            pltpu.VMEM((tb, lines, LANES), jnp.float32),
            pltpu.VMEM((lines, LANES), jnp.float32),
            pltpu.VMEM((tb, lines, LANES), jnp.float32),
            pltpu.VMEM((rows // LANES, LANES), jnp.float32),
            dma((n,)), dma((n,)), dma((tb,)), dma((tb,)),
            dma((n,)), dma((n,)), dma((tb,)), dma((tb,)),
            dma((4,)),
        ],
        compiler_params=pltpu.CompilerParams(collective_id=0, has_side_effects=True),
    )(
        gradients.reshape(tb, cols, count),
        row_ids.reshape(1, count),
        adagrad_state.reshape(rows // LANES, LANES),
        table_block,
    )
    return (new_table, new_state.reshape(rows))


def body(dp, tb, gradients, row_ids, table_block, adagrad_state):
    width = gradients.shape[0]
    cols, rows = table_block.shape
    fits = (
        cols % 16 == 0
        and rows % (tb * 8 * LANES) == 0
        and rows % (4 * LO * 4) == 0
        and dp & (dp - 1) == 0
        and tb & (tb - 1) == 0
        and tb % 4 == 0
        and rows // LO <= 256
        and row_ids.shape[0] == LANES
    )
    args = (gradients, row_ids, table_block, adagrad_state)
    if fits:
        return kernel_body(dp, tb, width, *args)
    return plain_body(width, *args)


def solution(mesh):
    in_specs = (P(None, ("dp", "table")), P(("dp", "table")), P("table", "dp"), P("dp"))
    out_specs = (P("table", "dp"), P("dp"))
    run = functools.partial(body, mesh.shape["dp"], mesh.shape["table"])
    return jax.shard_map(run, mesh=mesh, in_specs=in_specs, out_specs=out_specs, check_vma=False)
```

```python
import functools

import jax
import jax.numpy as jnp
from jax import lax
from jax.experimental import pallas as pl
from jax.experimental.pallas import tpu as pltpu
from jax.sharding import PartitionSpec as P

learn_rate = 0.5
LO = 256
LANES = 128
GROUP = 4
MESH = pl.DeviceIdType.MESH


def accumulate(grads, ids, first_row, count_rows):
    relative = ids - first_row
    inside = (relative >= 0) & (relative < count_rows)
    target = jnp.where(inside, relative, count_rows)
    start_total = jnp.zeros((grads.shape[0], count_rows), jnp.float32)
    return start_total.at[:, target].add(grads.astype(jnp.float32), mode="drop")


def plain_body(width, gradients, row_ids, table_block, adagrad_state):
    owned = lax.all_to_all(gradients, "table", split_axis=0, concat_axis=1, tiled=True)
    local_rows = table_block.shape[1]
    all_row_ids = lax.all_gather(row_ids, ("dp", "table"), axis=0, tiled=True)
    first_row = lax.axis_index("dp") * local_rows
    row_grad = accumulate(
        lax.all_gather(owned, "dp", axis=1, tiled=True), all_row_ids, first_row, local_rows
    )
    partial_squares = jnp.sum(row_grad * row_grad, axis=0)
    squares = lax.psum(partial_squares, "table")
    new_state = adagrad_state + squares / width
    new_table = table_block - learn_rate * row_grad / jnp.sqrt(new_state)[None, :]
    return (new_table, new_state)


def flips(value, size):
    table, bit = [value], 1
    while bit < size:
        change = bit - 2 * bit * lax.rem(value // bit, 2)
        table = table + [old + change for old in table]
        bit *= 2
    return table


def exchange_kernel(
    dp, tb, cols, rows, width,
    g_ref, id_ref, state_ref, table_ref, table_out, state_out,
    acc, got_g, got_i, table, part, red, total, full, state,
    send_g, send_i, send_r, send_a, recv_g, recv_i, recv_r, recv_a, own_sem,
):
    d, t = lax.axis_index("dp"), lax.axis_index("table")
    n = dp * tb
    me = d * tb + t
    his = rows // LO
    teams = tb // 2
    base = tb // 4
    lines = rows // teams // LANES
    parts = LO // LANES
    each = his // teams
    first_row = d * rows
    ts, ds = flips(t, tb), flips(d, dp)
    reducer = jnp.logical_and(t >= base, t < base + teams)

    def device(k):
        return ds[k // 4 % dp], ts[k % 4 + k // (4 * dp) * 4]

    barrier = pltpu.get_barrier_semaphore()
    for k in reversed(range(1, n)):
        pl.semaphore_signal(barrier, inc=1, device_id=device(k), device_id_type=MESH)

    own = (
        pltpu.make_async_copy(g_ref.at[t], got_g.at[me], own_sem.at[0]),
        pltpu.make_async_copy(id_ref, got_i.at[me], own_sem.at[1]),
        pltpu.make_async_copy(state_ref, state, own_sem.at[2]),
        pltpu.make_async_copy(table_ref, table, own_sem.at[3]),
    )
    for copy in own:
        copy.start()
    acc[...] = jnp.zeros_like(acc)
    pl.semaphore_wait(barrier, n - 1)

    def block_copies(k):
        to = device(k)
        return (
            pltpu.make_async_remote_copy(
                src_ref=id_ref, dst_ref=got_i.at[me],
                send_sem=send_i.at[k], recv_sem=recv_i.at[k],
                device_id=to, device_id_type=MESH,
            ),
            pltpu.make_async_remote_copy(
                src_ref=g_ref.at[to[1]], dst_ref=got_g.at[me],
                send_sem=send_g.at[k], recv_sem=recv_g.at[k],
                device_id=to, device_id_type=MESH,
            ),
        )

    for k in range(1, n):
        for copy in block_copies(k):
            copy.start()

    def arrived(k):
        there = device(k)
        source = there[0] * tb + there[1]
        pltpu.make_async_copy(id_ref, got_i.at[source], recv_i.at[k]).wait()
        pltpu.make_async_copy(g_ref.at[t], got_g.at[source], recv_g.at[k]).wait()
        return source

    def add(sources):
        ids = jnp.concatenate([got_i[k] for k in sources], axis=1) - first_row
        grads = jnp.concatenate([got_g[k] for k in sources], axis=1)
        span = ids.shape[1]
        low = jnp.broadcast_to(lax.bitwise_and(ids, LO - 1), (LO, span))
        place = lax.broadcasted_iota(jnp.int32, (LO, span), 0)
        one_hot = jnp.where(low == place, 1.0, 0.0).astype(jnp.bfloat16)
        high = jnp.broadcast_to(lax.shift_right_arithmetic(ids, 8), (cols, span))
        high = jnp.clip(high, -1, his).astype(jnp.float32).astype(jnp.bfloat16)
        zero = jnp.zeros_like(grads)
        picked = jnp.concatenate(
            [jnp.where(high == jnp.bfloat16(h), grads, zero) for h in range(his)], axis=0
        )
        acc[...] += lax.dot_general(
            picked, one_hot, (((1,), (1,)), ((), ())), preferred_element_type=jnp.float32
        )

    own[0].wait()
    own[1].wait()
    add([me] + [arrived(k) for k in range(1, GROUP)])
    for first in range(GROUP, n, GROUP):
        add([arrived(k) for k in range(first, first + GROUP)])

    for j in range(teams):
        pieces = []
        for h in range(each):
            at = (j * each + h) * cols
            piece = acc[at:at + cols, :]
            sums = jnp.sum(piece * piece, axis=0, keepdims=True)
            for half in range(parts):
                pieces.append(sums[:, half * LANES:(half + 1) * LANES])
        part[j] = jnp.concatenate(pieces, axis=0)

    def part_copy(k):
        team = lax.rem(t + (tb - base + k), teams)
        return pltpu.make_async_remote_copy(
            src_ref=part.at[team], dst_ref=red.at[t],
            send_sem=send_r.at[k], recv_sem=recv_r.at[t],
            device_id=(d, team + base), device_id_type=MESH,
        )

    for k in reversed(range(1, teams)):
        part_copy(k).start()

    @pl.when(jnp.logical_not(reducer))
    def _():
        part_copy(0).start()

    own[2].wait()
    own[3].wait()

    def total_copy(k):
        return pltpu.make_async_remote_copy(
            src_ref=total, dst_ref=full.at[t - base],
            send_sem=send_a.at[k], recv_sem=recv_a.at[t - base],
            device_id=(d, ts[k]), device_id_type=MESH,
        )

    @pl.when(reducer)
    def _():
        mine = t - base
        red[t] = part[mine]
        for k in range(1, tb):
            pltpu.make_async_copy(part.at[0], red.at[ts[k]], recv_r.at[ts[k]]).wait()
        here = pl.ds(pl.multiple_of(mine * lines, lines), lines)
        fresh = state[here, :] + jnp.sum(red[...], axis=0) / width
        total[...] = fresh
        full[mine] = fresh
        for k in range(1, teams):
            part_copy(k).wait_send()
        for k in reversed(range(1, tb)):
            total_copy(k).start()

    def update(j):
        fresh = full[j]
        state_out[j] = fresh
        scale = learn_rate / jnp.sqrt(fresh)
        for r in range(lines):
            h, half = r // parts, r % parts
            at = pl.multiple_of((j * each + h) * cols, cols)
            lanes = pl.ds(pl.multiple_of((j * lines + r) * LANES, LANES), LANES)
            step = acc[pl.ds(at, cols), half * LANES:(half + 1) * LANES]
            table_out[:, lanes] = table[:, lanes] - step * scale[r:r + 1, :]

    for k in range(1, n):
        for copy in block_copies(k):
            copy.wait_send()

    def receive(k):
        team = lax.rem(t + (tb - base + k), teams)
        pltpu.make_async_copy(total, full.at[team], recv_a.at[team]).wait()
        update(team)

    @pl.when(reducer)
    def _():
        update(t - base)

    @pl.when(jnp.logical_not(reducer))
    def _():
        receive(0)
        for k in range(teams):
            part_copy(k).wait_send()

    @pl.loop(1, teams)
    def _(k):
        receive(k)

    @pl.when(reducer)
    def _():
        for k in range(1, tb):
            total_copy(k).wait_send()


def kernel_body(dp, tb, width, gradients, row_ids, table_block, adagrad_state):
    cols, rows = table_block.shape
    count = row_ids.shape[0]
    n = dp * tb
    his = rows // LO
    teams = tb // 2
    lines = rows // teams // LANES
    dma = pltpu.SemaphoreType.DMA
    new_table, new_state = pl.pallas_call(
        functools.partial(exchange_kernel, dp, tb, cols, rows, width),
        name="exchange",
        out_shape=(
            pltpu.VMEM((cols, rows), jnp.float32),
            pltpu.VMEM((teams, lines, LANES), jnp.float32),
        ),
        in_specs=[pl.BlockSpec(memory_space=pl.ANY)] * 4,
        out_specs=(pl.BlockSpec(memory_space=pltpu.VMEM),) * 2,
        scratch_shapes=[
            pltpu.VMEM((his * cols, LO), jnp.float32),
            pltpu.VMEM((n, cols, count), jnp.bfloat16),
            pltpu.VMEM((n, 1, count), jnp.int32),
            pltpu.VMEM((cols, rows), jnp.float32),
            pltpu.VMEM((teams, lines, LANES), jnp.float32),
            pltpu.VMEM((tb, lines, LANES), jnp.float32),
            pltpu.VMEM((lines, LANES), jnp.float32),
            pltpu.VMEM((teams, lines, LANES), jnp.float32),
            pltpu.VMEM((rows // LANES, LANES), jnp.float32),
            dma((n,)), dma((n,)), dma((teams,)), dma((tb,)),
            dma((n,)), dma((n,)), dma((tb,)), dma((teams,)),
            dma((4,)),
        ],
        compiler_params=pltpu.CompilerParams(collective_id=0, has_side_effects=True),
    )(
        gradients.reshape(tb, cols, count),
        row_ids.reshape(1, count),
        adagrad_state.reshape(rows // LANES, LANES),
        table_block,
    )
    return (new_table, new_state.reshape(rows))


def body(dp, tb, gradients, row_ids, table_block, adagrad_state):
    width = gradients.shape[0]
    cols, rows = table_block.shape
    fits = (
        cols % 16 == 0
        and rows % (tb * 8 * LANES) == 0
        and rows % (4 * LO * 4) == 0
        and dp & (dp - 1) == 0
        and tb & (tb - 1) == 0
        and tb % 4 == 0
        and rows // LO <= 256
        and row_ids.shape[0] == LANES
    )
    args = (gradients, row_ids, table_block, adagrad_state)
    if fits:
        return kernel_body(dp, tb, width, *args)
    return plain_body(width, *args)


def solution(mesh):
    in_specs = (P(None, ("dp", "table")), P(("dp", "table")), P("table", "dp"), P("dp"))
    out_specs = (P("table", "dp"), P("dp"))
    run = functools.partial(body, mesh.shape["dp"], mesh.shape["table"])
    return jax.shard_map(run, mesh=mesh, in_specs=in_specs, out_specs=out_specs, check_vma=False)
```

```python
import functools

import jax
import jax.numpy as jnp
from jax import lax
from jax.experimental import pallas as pl
from jax.experimental.pallas import tpu as pltpu
from jax.sharding import PartitionSpec as P

learn_rate = 0.5
LO = 256
LANES = 128
GROUP = 4
PIECES = 4
MESH = pl.DeviceIdType.MESH


def accumulate(grads, ids, first_row, count_rows):
    relative = ids - first_row
    inside = (relative >= 0) & (relative < count_rows)
    target = jnp.where(inside, relative, count_rows)
    start_total = jnp.zeros((grads.shape[0], count_rows), jnp.float32)
    return start_total.at[:, target].add(grads.astype(jnp.float32), mode="drop")


def plain_body(width, gradients, row_ids, table_block, adagrad_state):
    owned = lax.all_to_all(gradients, "table", split_axis=0, concat_axis=1, tiled=True)
    local_rows = table_block.shape[1]
    all_row_ids = lax.all_gather(row_ids, ("dp", "table"), axis=0, tiled=True)
    first_row = lax.axis_index("dp") * local_rows
    row_grad = accumulate(
        lax.all_gather(owned, "dp", axis=1, tiled=True), all_row_ids, first_row, local_rows
    )
    partial_squares = jnp.sum(row_grad * row_grad, axis=0)
    squares = lax.psum(partial_squares, "table")
    new_state = adagrad_state + squares / width
    new_table = table_block - learn_rate * row_grad / jnp.sqrt(new_state)[None, :]
    return (new_table, new_state)


def flips(value, size):
    table, bit = [value], 1
    while bit < size:
        change = bit - 2 * bit * lax.rem(value // bit, 2)
        table = table + [old + change for old in table]
        bit *= 2
    return table


def exchange_kernel(
    dp, tb, cols, rows, width,
    g_ref, id_ref, state_ref, table_ref, table_out, state_out,
    acc, got_g, got_i, near_g, near_i, table, part, red, total, full, state,
    send_g, send_i, send_r, send_a, recv_g, recv_i, recv_r, recv_a, own_sem,
):
    d, t = lax.axis_index("dp"), lax.axis_index("table")
    n = dp * tb
    me = d * tb + t
    his = rows // LO
    teams = tb // 2
    base = tb // 4
    lines = rows // teams // LANES
    parts = LO // LANES
    each = his // teams
    first_row = d * rows
    ts, ds = flips(t, tb), flips(d, dp)
    reducer = jnp.logical_and(t >= base, t < base + teams)

    def device(k):
        return ds[k // 4 % dp], ts[k % 4 + k // (4 * dp) * 4]

    barrier = pltpu.get_barrier_semaphore()
    for k in reversed(range(1, n)):
        pl.semaphore_signal(barrier, inc=1, device_id=device(k), device_id_type=MESH)

    own = (
        pltpu.make_async_copy(g_ref, near_g, own_sem.at[0]),
        pltpu.make_async_copy(id_ref, near_i, own_sem.at[1]),
        pltpu.make_async_copy(state_ref, state, own_sem.at[2]),
        pltpu.make_async_copy(table_ref, table, own_sem.at[3]),
    )
    for copy in own:
        copy.start()
    acc[...] = jnp.zeros_like(acc)
    own[0].wait()
    own[1].wait()
    got_g[me] = near_g[t]
    got_i[me] = near_i[...]
    pl.semaphore_wait(barrier, n - 1)

    def block_copies(k):
        to = device(k)
        return (
            pltpu.make_async_remote_copy(
                src_ref=near_i, dst_ref=got_i.at[me],
                send_sem=send_i.at[k], recv_sem=recv_i.at[k],
                device_id=to, device_id_type=MESH,
            ),
            pltpu.make_async_remote_copy(
                src_ref=near_g.at[to[1]], dst_ref=got_g.at[me],
                send_sem=send_g.at[k], recv_sem=recv_g.at[k],
                device_id=to, device_id_type=MESH,
            ),
        )

    for k in range(1, n):
        for copy in block_copies(k):
            copy.start()

    def arrived(k):
        there = device(k)
        source = there[0] * tb + there[1]
        pltpu.make_async_copy(near_i, got_i.at[source], recv_i.at[k]).wait()
        pltpu.make_async_copy(near_g.at[t], got_g.at[source], recv_g.at[k]).wait()
        return source

    def add(sources):
        ids = jnp.concatenate([got_i[k] for k in sources], axis=1) - first_row
        grads = jnp.concatenate([got_g[k] for k in sources], axis=1)
        span = ids.shape[1]
        low = jnp.broadcast_to(lax.bitwise_and(ids, LO - 1), (LO, span))
        place = lax.broadcasted_iota(jnp.int32, (LO, span), 0)
        one_hot = jnp.where(low == place, 1.0, 0.0).astype(jnp.bfloat16)
        high = jnp.broadcast_to(lax.shift_right_arithmetic(ids, 8), (cols, span))
        high = jnp.clip(high, -1, his).astype(jnp.float32).astype(jnp.bfloat16)
        zero = jnp.zeros_like(grads)
        picked = jnp.concatenate(
            [jnp.where(high == jnp.bfloat16(h), grads, zero) for h in range(his)], axis=0
        )
        acc[...] += lax.dot_general(
            picked, one_hot, (((1,), (1,)), ((), ())), preferred_element_type=jnp.float32
        )

    add([me] + [arrived(k) for k in range(1, GROUP)])
    for first in range(GROUP, n, GROUP):
        add([arrived(k) for k in range(first, first + GROUP)])

    for j in range(teams):
        pieces = []
        for h in range(each):
            at = (j * each + h) * cols
            piece = acc[at:at + cols, :]
            sums = jnp.sum(piece * piece, axis=0, keepdims=True)
            for half in range(parts):
                pieces.append(sums[:, half * LANES:(half + 1) * LANES])
        part[j] = jnp.concatenate(pieces, axis=0)

    def part_copy(k):
        team = lax.rem(t + (tb - base + k), teams)
        return pltpu.make_async_remote_copy(
            src_ref=part.at[team], dst_ref=red.at[t],
            send_sem=send_r.at[k], recv_sem=recv_r.at[t],
            device_id=(d, team + base), device_id_type=MESH,
        )

    for k in reversed(range(1, teams)):
        part_copy(k).start()

    @pl.when(jnp.logical_not(reducer))
    def _():
        part_copy(0).start()

    own[2].wait()
    own[3].wait()

    def total_copy(k):
        return pltpu.make_async_remote_copy(
            src_ref=total, dst_ref=full.at[t - base],
            send_sem=send_a.at[k], recv_sem=recv_a.at[t - base],
            device_id=(d, ts[k]), device_id_type=MESH,
        )

    @pl.when(reducer)
    def _():
        mine = t - base
        red[t] = part[mine]
        for k in range(1, tb):
            pltpu.make_async_copy(part.at[0], red.at[ts[k]], recv_r.at[ts[k]]).wait()
        here = pl.ds(pl.multiple_of(mine * lines, lines), lines)
        fresh = state[here, :] + jnp.sum(red[...], axis=0) / width
        total[...] = fresh
        full[mine] = fresh
        for k in range(1, teams):
            part_copy(k).wait_send()
        for k in reversed(range(1, tb)):
            total_copy(k).start()

    def update(j):
        fresh = full[j]
        state_out[j] = fresh
        scale = learn_rate / jnp.sqrt(fresh)
        for r in range(lines):
            h, half = r // parts, r % parts
            at = pl.multiple_of((j * each + h) * cols, cols)
            lanes = pl.ds(pl.multiple_of((j * lines + r) * LANES, LANES), LANES)
            step = acc[pl.ds(at, cols), half * LANES:(half + 1) * LANES]
            table_out[:, lanes] = table[:, lanes] - step * scale[r:r + 1, :]

    for k in range(1, n):
        for copy in block_copies(k):
            copy.wait_send()

    def receive(k):
        team = lax.rem(t + (tb - base + k), teams)
        pltpu.make_async_copy(total, full.at[team], recv_a.at[team]).wait()
        update(team)

    @pl.when(reducer)
    def _():
        update(t - base)

    @pl.when(jnp.logical_not(reducer))
    def _():
        receive(0)
        for k in range(teams):
            part_copy(k).wait_send()

    @pl.loop(1, teams)
    def _(k):
        receive(k)

    @pl.when(reducer)
    def _():
        for k in range(1, tb):
            total_copy(k).wait_send()


def finish_kernel(table_ref, state_ref, table_out, state_out, sems):
    rows = table_ref.shape[1]
    size = rows // PIECES
    copies = [
        pltpu.make_async_copy(
            table_ref.at[:, pl.ds(p * size, size)], table_out.at[:, pl.ds(p * size, size)], sems.at[p]
        )
        for p in range(PIECES)
    ]
    copies.append(pltpu.make_async_copy(state_ref, state_out, sems.at[PIECES]))
    for copy in copies:
        copy.start()
    for copy in copies:
        copy.wait()


def kernel_body(dp, tb, width, gradients, row_ids, table_block, adagrad_state):
    cols, rows = table_block.shape
    count = row_ids.shape[0]
    n = dp * tb
    his = rows // LO
    teams = tb // 2
    lines = rows // teams // LANES
    dma = pltpu.SemaphoreType.DMA
    new_table, new_state = pl.pallas_call(
        functools.partial(exchange_kernel, dp, tb, cols, rows, width),
        name="exchange",
        out_shape=(
            pltpu.VMEM((cols, rows), jnp.float32),
            pltpu.VMEM((teams, lines, LANES), jnp.float32),
        ),
        in_specs=[pl.BlockSpec(memory_space=pl.ANY)] * 4,
        out_specs=(pl.BlockSpec(memory_space=pltpu.VMEM),) * 2,
        scratch_shapes=[
            pltpu.VMEM((his * cols, LO), jnp.float32),
            pltpu.VMEM((n, cols, count), jnp.bfloat16),
            pltpu.VMEM((n, 1, count), jnp.int32),
            pltpu.VMEM((tb, cols, count), jnp.bfloat16),
            pltpu.VMEM((1, count), jnp.int32),
            pltpu.VMEM((cols, rows), jnp.float32),
            pltpu.VMEM((teams, lines, LANES), jnp.float32),
            pltpu.VMEM((tb, lines, LANES), jnp.float32),
            pltpu.VMEM((lines, LANES), jnp.float32),
            pltpu.VMEM((teams, lines, LANES), jnp.float32),
            pltpu.VMEM((rows // LANES, LANES), jnp.float32),
            dma((n,)), dma((n,)), dma((teams,)), dma((tb,)),
            dma((n,)), dma((n,)), dma((tb,)), dma((teams,)),
            dma((4,)),
        ],
        compiler_params=pltpu.CompilerParams(collective_id=0, has_side_effects=True),
    )(
        gradients.reshape(tb, cols, count),
        row_ids.reshape(1, count),
        adagrad_state.reshape(rows // LANES, LANES),
        table_block,
    )
    new_table, new_state = pl.pallas_call(
        finish_kernel,
        name="finish",
        out_shape=(
            jax.ShapeDtypeStruct((cols, rows), jnp.float32),
            jax.ShapeDtypeStruct((teams, lines, LANES), jnp.float32),
        ),
        in_specs=[pl.BlockSpec(memory_space=pltpu.VMEM)] * 2,
        out_specs=(pl.BlockSpec(memory_space=pl.ANY),) * 2,
        scratch_shapes=[dma((PIECES + 1,))],
    )(
        pltpu.with_memory_space_constraint(new_table, pltpu.VMEM),
        pltpu.with_memory_space_constraint(new_state, pltpu.VMEM),
    )
    return (new_table, new_state.reshape(rows))


def body(dp, tb, gradients, row_ids, table_block, adagrad_state):
    width = gradients.shape[0]
    cols, rows = table_block.shape
    fits = (
        cols % 16 == 0
        and rows % (tb * 8 * LANES) == 0
        and rows % (4 * LO * 4) == 0
        and dp & (dp - 1) == 0
        and tb & (tb - 1) == 0
        and tb % 4 == 0
        and rows // LO <= 256
        and row_ids.shape[0] == LANES
    )
    args = (gradients, row_ids, table_block, adagrad_state)
    if fits:
        return kernel_body(dp, tb, width, *args)
    return plain_body(width, *args)


def solution(mesh):
    in_specs = (P(None, ("dp", "table")), P(("dp", "table")), P("table", "dp"), P("dp"))
    out_specs = (P("table", "dp"), P("dp"))
    run = functools.partial(body, mesh.shape["dp"], mesh.shape["table"])
    return jax.shard_map(run, mesh=mesh, in_specs=in_specs, out_specs=out_specs, check_vma=False)
```

```python
import functools

import jax
import jax.numpy as jnp
from jax import lax
from jax.experimental import pallas as pl
from jax.experimental.pallas import tpu as pltpu
from jax.sharding import PartitionSpec as P

learn_rate = 0.5
LO = 256
LANES = 128
GROUP = 4
PIECES = 4
MESH = pl.DeviceIdType.MESH


def accumulate(grads, ids, first_row, count_rows):
    relative = ids - first_row
    inside = (relative >= 0) & (relative < count_rows)
    target = jnp.where(inside, relative, count_rows)
    start_total = jnp.zeros((grads.shape[0], count_rows), jnp.float32)
    return start_total.at[:, target].add(grads.astype(jnp.float32), mode="drop")


def plain_body(width, gradients, row_ids, table_block, adagrad_state):
    owned = lax.all_to_all(gradients, "table", split_axis=0, concat_axis=1, tiled=True)
    local_rows = table_block.shape[1]
    all_row_ids = lax.all_gather(row_ids, ("dp", "table"), axis=0, tiled=True)
    first_row = lax.axis_index("dp") * local_rows
    row_grad = accumulate(
        lax.all_gather(owned, "dp", axis=1, tiled=True), all_row_ids, first_row, local_rows
    )
    partial_squares = jnp.sum(row_grad * row_grad, axis=0)
    squares = lax.psum(partial_squares, "table")
    new_state = adagrad_state + squares / width
    new_table = table_block - learn_rate * row_grad / jnp.sqrt(new_state)[None, :]
    return (new_table, new_state)


def flips(value, size):
    table, bit = [value], 1
    while bit < size:
        change = bit - 2 * bit * lax.rem(value // bit, 2)
        table = table + [old + change for old in table]
        bit *= 2
    return table


def exchange_kernel(
    dp, tb, cols, rows, width,
    g_ref, id_ref, state_ref, table_ref, table_out, state_out,
    acc, got_g, got_i, near_g, near_i, table, part, red, total, full, state,
    send_g, send_i, send_r, send_a, recv_g, recv_i, recv_r, recv_a, own_sem,
):
    d, t = lax.axis_index("dp"), lax.axis_index("table")
    n = dp * tb
    me = d * tb + t
    his = rows // LO
    teams = tb
    base = 0
    lines = rows // teams // LANES
    parts = LO // LANES
    each = his // teams
    first_row = d * rows
    ts, ds = flips(t, tb), flips(d, dp)
    reducer = jnp.logical_and(t >= base, t < base + teams)

    def device(k):
        return ds[k // 4 % dp], ts[k % 4 + k // (4 * dp) * 4]

    barrier = pltpu.get_barrier_semaphore()
    for k in reversed(range(1, n)):
        pl.semaphore_signal(barrier, inc=1, device_id=device(k), device_id_type=MESH)

    own = (
        pltpu.make_async_copy(g_ref, near_g, own_sem.at[0]),
        pltpu.make_async_copy(id_ref, near_i, own_sem.at[1]),
        pltpu.make_async_copy(state_ref, state, own_sem.at[2]),
        pltpu.make_async_copy(table_ref, table, own_sem.at[3]),
    )
    for copy in own:
        copy.start()
    acc[...] = jnp.zeros_like(acc)
    own[0].wait()
    own[1].wait()
    got_g[me] = near_g[t]
    got_i[me] = near_i[...]
    pl.semaphore_wait(barrier, n - 1)

    def block_copies(k):
        to = device(k)
        return (
            pltpu.make_async_remote_copy(
                src_ref=near_i, dst_ref=got_i.at[me],
                send_sem=send_i.at[k], recv_sem=recv_i.at[k],
                device_id=to, device_id_type=MESH,
            ),
            pltpu.make_async_remote_copy(
                src_ref=near_g.at[to[1]], dst_ref=got_g.at[me],
                send_sem=send_g.at[k], recv_sem=recv_g.at[k],
                device_id=to, device_id_type=MESH,
            ),
        )

    for k in range(1, n):
        for copy in block_copies(k):
            copy.start()

    def arrived(k):
        there = device(k)
        source = there[0] * tb + there[1]
        pltpu.make_async_copy(near_i, got_i.at[source], recv_i.at[k]).wait()
        pltpu.make_async_copy(near_g.at[t], got_g.at[source], recv_g.at[k]).wait()
        return source

    def add(sources):
        ids = jnp.concatenate([got_i[k] for k in sources], axis=1) - first_row
        grads = jnp.concatenate([got_g[k] for k in sources], axis=1)
        span = ids.shape[1]
        low = jnp.broadcast_to(lax.bitwise_and(ids, LO - 1), (LO, span))
        place = lax.broadcasted_iota(jnp.int32, (LO, span), 0)
        one_hot = jnp.where(low == place, 1.0, 0.0).astype(jnp.bfloat16)
        high = jnp.broadcast_to(lax.shift_right_arithmetic(ids, 8), (cols, span))
        high = jnp.clip(high, -1, his).astype(jnp.float32).astype(jnp.bfloat16)
        zero = jnp.zeros_like(grads)
        picked = jnp.concatenate(
            [jnp.where(high == jnp.bfloat16(h), grads, zero) for h in range(his)], axis=0
        )
        acc[...] += lax.dot_general(
            picked, one_hot, (((1,), (1,)), ((), ())), preferred_element_type=jnp.float32
        )

    add([me] + [arrived(k) for k in range(1, GROUP)])
    for first in range(GROUP, n, GROUP):
        add([arrived(k) for k in range(first, first + GROUP)])

    for j in range(teams):
        pieces = []
        for h in range(each):
            at = (j * each + h) * cols
            piece = acc[at:at + cols, :]
            sums = jnp.sum(piece * piece, axis=0, keepdims=True)
            for half in range(parts):
                pieces.append(sums[:, half * LANES:(half + 1) * LANES])
        part[j] = jnp.concatenate(pieces, axis=0)

    def part_copy(k):
        team = ts[k]
        return pltpu.make_async_remote_copy(
            src_ref=part.at[team], dst_ref=red.at[t],
            send_sem=send_r.at[k], recv_sem=recv_r.at[t],
            device_id=(d, team + base), device_id_type=MESH,
        )

    for k in reversed(range(1, teams)):
        part_copy(k).start()

    own[2].wait()
    own[3].wait()

    def total_copy(k):
        return pltpu.make_async_remote_copy(
            src_ref=total, dst_ref=full.at[t - base],
            send_sem=send_a.at[k], recv_sem=recv_a.at[t - base],
            device_id=(d, ts[k]), device_id_type=MESH,
        )

    @pl.when(reducer)
    def _():
        mine = t - base
        red[t] = part[mine]
        for k in range(1, tb):
            pltpu.make_async_copy(part.at[0], red.at[ts[k]], recv_r.at[ts[k]]).wait()
        here = pl.ds(pl.multiple_of(mine * lines, lines), lines)
        fresh = state[here, :] + jnp.sum(red[...], axis=0) / width
        total[...] = fresh
        full[mine] = fresh
        for k in range(1, teams):
            part_copy(k).wait_send()
        for k in reversed(range(1, tb)):
            total_copy(k).start()

    def update(j):
        fresh = full[j]
        state_out[j] = fresh
        scale = learn_rate / jnp.sqrt(fresh)
        for r in range(lines):
            h, half = r // parts, r % parts
            at = pl.multiple_of((j * each + h) * cols, cols)
            lanes = pl.ds(pl.multiple_of((j * lines + r) * LANES, LANES), LANES)
            step = acc[pl.ds(at, cols), half * LANES:(half + 1) * LANES]
            table_out[:, lanes] = table[:, lanes] - step * scale[r:r + 1, :]

    for k in range(1, n):
        for copy in block_copies(k):
            copy.wait_send()

    def receive(k):
        team = lax.rem(t + (tb - base + k), teams)
        pltpu.make_async_copy(total, full.at[team], recv_a.at[team]).wait()
        update(team)

    @pl.when(reducer)
    def _():
        update(t - base)

    @pl.loop(1, teams)
    def _(k):
        receive(k)

    @pl.when(reducer)
    def _():
        for k in range(1, tb):
            total_copy(k).wait_send()


def finish_kernel(table_ref, state_ref, table_out, state_out, sems):
    rows = table_ref.shape[1]
    size = rows // PIECES
    copies = [
        pltpu.make_async_copy(
            table_ref.at[:, pl.ds(p * size, size)], table_out.at[:, pl.ds(p * size, size)], sems.at[p]
        )
        for p in range(PIECES)
    ]
    copies.append(pltpu.make_async_copy(state_ref, state_out, sems.at[PIECES]))
    for copy in copies:
        copy.start()
    for copy in copies:
        copy.wait()


def kernel_body(dp, tb, width, gradients, row_ids, table_block, adagrad_state):
    cols, rows = table_block.shape
    count = row_ids.shape[0]
    n = dp * tb
    his = rows // LO
    teams = tb
    lines = rows // teams // LANES
    dma = pltpu.SemaphoreType.DMA
    new_table, new_state = pl.pallas_call(
        functools.partial(exchange_kernel, dp, tb, cols, rows, width),
        name="exchange",
        out_shape=(
            pltpu.VMEM((cols, rows), jnp.float32),
            pltpu.VMEM((teams, lines, LANES), jnp.float32),
        ),
        in_specs=[pl.BlockSpec(memory_space=pl.ANY)] * 4,
        out_specs=(pl.BlockSpec(memory_space=pltpu.VMEM),) * 2,
        scratch_shapes=[
            pltpu.VMEM((his * cols, LO), jnp.float32),
            pltpu.VMEM((n, cols, count), jnp.bfloat16),
            pltpu.VMEM((n, 1, count), jnp.int32),
            pltpu.VMEM((tb, cols, count), jnp.bfloat16),
            pltpu.VMEM((1, count), jnp.int32),
            pltpu.VMEM((cols, rows), jnp.float32),
            pltpu.VMEM((teams, lines, LANES), jnp.float32),
            pltpu.VMEM((tb, lines, LANES), jnp.float32),
            pltpu.VMEM((lines, LANES), jnp.float32),
            pltpu.VMEM((teams, lines, LANES), jnp.float32),
            pltpu.VMEM((rows // LANES, LANES), jnp.float32),
            dma((n,)), dma((n,)), dma((teams,)), dma((tb,)),
            dma((n,)), dma((n,)), dma((tb,)), dma((teams,)),
            dma((4,)),
        ],
        compiler_params=pltpu.CompilerParams(collective_id=0, has_side_effects=True),
    )(
        gradients.reshape(tb, cols, count),
        row_ids.reshape(1, count),
        adagrad_state.reshape(rows // LANES, LANES),
        table_block,
    )
    new_table, new_state = pl.pallas_call(
        finish_kernel,
        name="finish",
        out_shape=(
            jax.ShapeDtypeStruct((cols, rows), jnp.float32),
            jax.ShapeDtypeStruct((teams, lines, LANES), jnp.float32),
        ),
        in_specs=[pl.BlockSpec(memory_space=pltpu.VMEM)] * 2,
        out_specs=(pl.BlockSpec(memory_space=pl.ANY),) * 2,
        scratch_shapes=[dma((PIECES + 1,))],
    )(
        pltpu.with_memory_space_constraint(new_table, pltpu.VMEM),
        pltpu.with_memory_space_constraint(new_state, pltpu.VMEM),
    )
    return (new_table, new_state.reshape(rows))


def body(dp, tb, gradients, row_ids, table_block, adagrad_state):
    width = gradients.shape[0]
    cols, rows = table_block.shape
    fits = (
        cols % 16 == 0
        and rows % (tb * 8 * LANES) == 0
        and rows % (4 * LO * 4) == 0
        and dp & (dp - 1) == 0
        and tb & (tb - 1) == 0
        and tb % 4 == 0
        and rows // LO <= 256
        and row_ids.shape[0] == LANES
    )
    args = (gradients, row_ids, table_block, adagrad_state)
    if fits:
        return kernel_body(dp, tb, width, *args)
    return plain_body(width, *args)


def solution(mesh):
    in_specs = (P(None, ("dp", "table")), P(("dp", "table")), P("table", "dp"), P("dp"))
    out_specs = (P("table", "dp"), P("dp"))
    run = functools.partial(body, mesh.shape["dp"], mesh.shape["table"])
    return jax.shard_map(run, mesh=mesh, in_specs=in_specs, out_specs=out_specs, check_vma=False)
```
